32 devices in a mesh: dp: 2 (over core), seq: 4 (over z), head: 4 (over y, x).
Axes of the slice: x: 2, y: 2, z: 4, core: 2. Of those that a mesh axis runs over, the one named last changes fastest.
Arguments:
- x_in: float32 [2, 512, 1024], P('dp', 'seq'), may hold values from -6 to 6
- cotangent: float32 [2, 512, 1024], P('dp', 'seq'), may hold values from -6 to 6
- attn_gain: bfloat16 [1024], P('seq'), may hold values from 0.25 to 1.75
- w_query: bfloat16 [1024, 512], P('seq', 'head'), may hold values from -0.1875 to 0.1875
- w_key: bfloat16 [1024, 512], P('seq', 'head'), may hold values from -0.1875 to 0.1875
- w_value: bfloat16 [1024, 1024], P('seq', 'head'), may hold values from -0.1875 to 0.1875
- w_outgate: bfloat16 [1024, 1024], P('seq', 'head'), may hold values from -0.1875 to 0.1875
- w_lowrank: bfloat16 [1024, 16], P('seq'), may hold values from -0.1875 to 0.1875
- w_forget: float32 [16, 512], replicated, may hold values from -1.5 to 1.5
- forget_bias: float32 [512], replicated, may hold values from -1 to 6
- group_gain: float32 [256], replicated, may hold values from 0.25 to 1.75
- w_output: bfloat16 [1024, 1024], P('head', 'seq'), may hold values from -0.375 to 0.375
- mlp_gain: bfloat16 [1024], P('seq'), may hold values from 0.25 to 1.75
- w_gate: bfloat16 [1024, 2816], P('seq', 'head'), may hold values from -0.1875 to 0.1875
- w_up: bfloat16 [1024, 2816], P('seq', 'head'), may hold values from -0.1875 to 0.1875
- w_down: bfloat16 [2816, 1024], P('head', 'seq'), may hold values from -0.109375 to 0.109375
Outputs:
- block_out: float32 [2, 512, 1024], P('dp', 'seq')
- grad_input: float32 [2, 512, 1024], P('dp', 'seq')
- grad_attn_gain: float32 [1024], P('seq')
- grad_query: float32 [1024, 512], P('seq', 'head')
- grad_key: float32 [1024, 512], P('seq', 'head')
- grad_value: float32 [1024, 1024], P('seq', 'head')
- grad_outgate: float32 [1024, 1024], P('seq', 'head')
- grad_lowrank: float32 [1024, 16], P('seq')
- grad_forget: float32 [16, 512], replicated
- grad_bias: float32 [512], replicated
- grad_group_gain: float32 [256], replicated
- grad_output: float32 [1024, 1024], P('head', 'seq')
- grad_mlp_gain: float32 [1024], P('seq')
- grad_gate: float32 [1024, 2816], P('seq', 'head')
- grad_up: float32 [1024, 2816], P('seq', 'head')
- grad_down: float32 [2816, 1024], P('head', 'seq')
The draws below stay inside these ranges and needn't reach their ends.
All inputs are finite; a program needn't handle non-finite values.
Results may differ from the reference program's by a relative error of at most 0.0097.
Values may be sent and summed in bfloat16 or wider, within the bound.
A program may use at most 128 MiB of HBM per device.

```python
import jax
import jax.numpy as jnp
from jax import lax

D = 1024
H = 4
DK = 128
DV = 256
R = 16
FF = 2816
SPAN = 64
LEN = 512
SEQS = 2


def shard_levels(stream_key, shape, split, low, high):
    def one(axis_at, blocks):
        draws = jax.random.uniform(jax.random.fold_in(jax.random.fold_in(stream_key, 6), axis_at), (blocks,), jnp.float32, low / len(split), high / len(split))
        return jnp.repeat(jnp.exp(draws), shape[axis_at] // blocks).reshape((-1,) + (1,) * (len(shape) - axis_at - 1))

    level = one(*split[0])
    for cut in split[1:]:
        level = level * one(*cut)
    return level


def normal_values(own_key, extent, width, most, shards=(), held_as=jnp.bfloat16):
    drawn = width * jax.random.normal(own_key, extent, jnp.float32)
    if shards:
        drawn = drawn * shard_levels(own_key, extent, shards, -0.22, 0.18)
    return jnp.clip(drawn, -most, most).astype(held_as)


def setup_inputs(seed: int = 0) -> dict:
    streams_of = jax.random.split(jax.random.key(seed), 17)
    x_in = normal_values(streams_of[0], (SEQS, LEN, D), 1.0, 6.0, ((0, 2), (1, 4)), jnp.float32)
    cotangent = normal_values(streams_of[1], (SEQS, LEN, D), 1.0, 6.0, ((0, 2), (1, 4)), jnp.float32)
    attn_gain = jnp.clip(1.0 + 0.15 * jax.random.normal(streams_of[2], (D,), jnp.float32), 0.25, 1.75).astype(jnp.bfloat16)
    w_query = normal_values(streams_of[3], (D, H * DK), D ** -0.5, 0.1875, ((0, 4), (1, 4)))
    w_key = normal_values(streams_of[4], (D, H * DK), D ** -0.5, 0.1875, ((0, 4), (1, 4)))
    w_value = normal_values(streams_of[5], (D, H * DV), D ** -0.5, 0.1875, ((0, 4), (1, 4)))
    w_outgate = normal_values(streams_of[6], (D, H * DV), D ** -0.5, 0.1875, ((0, 4), (1, 4)))
    w_lowrank = normal_values(streams_of[7], (D, R), D ** -0.5, 0.1875, ((0, 4),))
    w_forget = normal_values(streams_of[8], (R, H * DK), R ** -0.5, 1.5, (), jnp.float32)
    forget_bias = jnp.clip(jax.random.uniform(streams_of[9], (H * DK,), jnp.float32, -1.0, 6.0), -1.0, 6.0)
    group_gain = jnp.clip(1.0 + 0.15 * jax.random.normal(streams_of[10], (DV,), jnp.float32), 0.25, 1.75)
    w_output = normal_values(streams_of[11], (H * DV, D), DV ** -0.5, 0.375, ((0, 4), (1, 4)))
    mlp_gain = jnp.clip(1.0 + 0.15 * jax.random.normal(streams_of[12], (D,), jnp.float32), 0.25, 1.75).astype(jnp.bfloat16)
    w_gate = normal_values(streams_of[13], (D, FF), D ** -0.5, 0.1875, ((0, 4), (1, 4)))
    w_up = normal_values(streams_of[14], (D, FF), D ** -0.5, 0.1875, ((0, 4), (1, 4)))
    w_down = normal_values(streams_of[15], (FF, D), FF ** -0.5, 0.109375, ((0, 4), (1, 4)))
    return dict(x_in=x_in, cotangent=cotangent, attn_gain=attn_gain, w_query=w_query, w_key=w_key, w_value=w_value, w_outgate=w_outgate, w_lowrank=w_lowrank, w_forget=w_forget, forget_bias=forget_bias, group_gain=group_gain, w_output=w_output, mlp_gain=mlp_gain, w_gate=w_gate, w_up=w_up, w_down=w_down)


epsilon = 1e-06
normalizer = 16.0
highest = lax.Precision.HIGHEST

def product(left, right):
    return jnp.dot(left, right, preferred_element_type=jnp.float32)

def rms_rows(inputs):
    return lax.rsqrt(lax.optimization_barrier(jnp.mean(inputs * inputs, axis=-1, keepdims=True)) + epsilon)

def norm_back(inputs, scale, gain, grad):
    scaled = gain * grad
    gain_terms = grad * inputs * scale
    input_grad = scale * scaled - inputs * scale ** 3 * lax.optimization_barrier(jnp.mean(scaled * inputs, axis=-1, keepdims=True))
    return (gain_terms, input_grad)

def mixer_block(queries, keys_in, values_in, log_decay, start_state):
    blocks = queries.shape[0] // SPAN

    def cut(array):
        return array.reshape(blocks, SPAN, array.shape[-1])
    lower = jnp.tril(jnp.ones((SPAN, SPAN), jnp.float32))

    def block_step(carried, pieces):
        query_blk, key_blk, value_blk, decay_blk = pieces
        running = jnp.cumsum(decay_blk, axis=0)
        from_state = jnp.dot(query_blk * jnp.exp(running), carried, precision=highest)
        spread = jnp.exp(jnp.minimum(running[:, None, :] - running[None, :, :], 0.0)) * lower[:, :, None]
        scores = jnp.einsum('id,jd,ijd->ij', query_blk, key_blk, spread, precision=highest)
        inside = jnp.dot(scores, value_blk, precision=highest)
        ending = running[-1]
        weighted = key_blk * jnp.exp(ending[None, :] - running)
        carried = jnp.exp(ending)[:, None] * carried + jnp.dot(weighted.T, value_blk, precision=highest)
        return (carried, from_state + inside)
    final_state, outputs = lax.scan(jax.checkpoint(block_step), start_state, (cut(queries), cut(keys_in), cut(values_in), cut(log_decay)))
    return (outputs.reshape(queries.shape[0], values_in.shape[-1]), final_state)

def reference(x_in, cotangent, attn_gain, w_query, w_key, w_value, w_outgate, w_lowrank, w_forget, forget_bias, group_gain, w_output, mlp_gain, w_gate, w_up, w_down):
    head_scale = DK ** (-0.5)
    gain_first = attn_gain.astype(jnp.float32)
    gain_second = mlp_gain.astype(jnp.float32)

    def one_sequence(totals, pair):
        seq_in, seq_cot = pair
        length = seq_in.shape[0]

        def heads_of(array, size):
            return array.reshape(length, H, size).transpose(1, 0, 2)

        def rows_of(array):
            return array.transpose(1, 0, 2).reshape(length, -1)
        scale_one = rms_rows(seq_in)
        normed_in = (seq_in * scale_one * gain_first).astype(jnp.bfloat16)
        q_rows = product(normed_in, w_query)
        k_rows = product(normed_in, w_key)
        v_rows = product(normed_in, w_value)
        og_rows = product(normed_in, w_outgate)
        low_rank = product(normed_in, w_lowrank)
        pre_gate = jnp.dot(low_rank, w_forget, precision=highest) + forget_bias
        log_decay = jax.nn.log_sigmoid(pre_gate) / normalizer

        def mixed(q_heads, k_heads, v_heads, d_heads):
            zero_state = jnp.zeros((H, DK, DV), jnp.float32)
            return jax.vmap(mixer_block)(q_heads * head_scale, k_heads, v_heads, d_heads, zero_state)
        (o_heads, end_state), pullback = jax.vjp(mixed, heads_of(q_rows, DK), heads_of(k_rows, DK), heads_of(v_rows, DV), heads_of(log_decay, DK))
        gate_heads = heads_of(og_rows, DV)
        scale_three = rms_rows(o_heads)
        gated_norm = o_heads * scale_three * group_gain
        gate_sig = jax.nn.sigmoid(gate_heads)
        gate_act = gate_heads * gate_sig
        mixed_out = rows_of(gated_norm * gate_act).astype(jnp.bfloat16)
        resid = seq_in + product(mixed_out, w_output)
        scale_two = rms_rows(resid)
        normed_mid = (resid * scale_two * gain_second).astype(jnp.bfloat16)
        gate_pre = product(normed_mid, w_gate)
        up_pre = product(normed_mid, w_up)
        gate_sigma = jax.nn.sigmoid(gate_pre)
        gate_silu = gate_pre * gate_sigma
        mlp_hidden = (gate_silu * up_pre).astype(jnp.bfloat16)
        result = resid + product(mlp_hidden, w_down)
        grad_out_b = seq_cot.astype(jnp.bfloat16)
        d_down = product(mlp_hidden.T, grad_out_b)
        d_hidden = product(grad_out_b, w_down.T)
        d_gate_pre = (d_hidden * up_pre * gate_sigma * (1.0 + gate_pre * (1.0 - gate_sigma))).astype(jnp.bfloat16)
        d_up_pre = (d_hidden * gate_silu).astype(jnp.bfloat16)
        d_gate = product(normed_mid.T, d_gate_pre)
        d_up = product(normed_mid.T, d_up_pre)
        d_normed_mid = product(d_gate_pre, w_gate.T) + product(d_up_pre, w_up.T)
        gain_terms, d_resid_norm = norm_back(resid, scale_two, gain_second, d_normed_mid)
        d_gain_two = lax.optimization_barrier(jnp.sum(gain_terms, axis=0))
        d_resid = seq_cot + d_resid_norm
        d_resid_b = d_resid.astype(jnp.bfloat16)
        d_output = product(mixed_out.T, d_resid_b)
        d_mixed = heads_of(product(d_resid_b, w_output.T), DV)
        d_norm_out = d_mixed * gate_act
        d_gate_heads = d_mixed * gated_norm * gate_sig * (1.0 + gate_heads * (1.0 - gate_sig))
        d_group = lax.optimization_barrier(jnp.sum(d_norm_out * o_heads * scale_three, axis=(0, 1)))
        group_terms, d_o_heads = norm_back(o_heads, scale_three, group_gain, d_norm_out)
        d_q, d_k, d_v, d_decay = pullback((d_o_heads, jnp.zeros_like(end_state)))
        d_pre = rows_of(d_decay) / normalizer * jax.nn.sigmoid(-pre_gate)
        d_bias = lax.optimization_barrier(jnp.sum(d_pre, axis=0))
        d_forget = jnp.dot(low_rank.T, d_pre, precision=highest)
        d_low_b = jnp.dot(d_pre, w_forget.T, precision=highest).astype(jnp.bfloat16)
        d_q_b = rows_of(d_q).astype(jnp.bfloat16)
        d_k_b = rows_of(d_k).astype(jnp.bfloat16)
        d_v_b = rows_of(d_v).astype(jnp.bfloat16)
        d_og_b = rows_of(d_gate_heads).astype(jnp.bfloat16)
        d_query = product(normed_in.T, d_q_b)
        d_key = product(normed_in.T, d_k_b)
        d_value = product(normed_in.T, d_v_b)
        d_outgate = product(normed_in.T, d_og_b)
        d_lowrank = product(normed_in.T, d_low_b)
        d_normed_in = product(d_q_b, w_query.T) + product(d_k_b, w_key.T) + product(d_v_b, w_value.T) + product(d_og_b, w_outgate.T) + product(d_low_b, w_lowrank.T)
        first_terms, d_in_norm = norm_back(seq_in, scale_one, gain_first, d_normed_in)
        d_gain_one = lax.optimization_barrier(jnp.sum(first_terms, axis=0))
        grad_in = d_resid + d_in_norm
        grads = (d_gain_one, d_query, d_key, d_value, d_outgate, d_lowrank, d_forget, d_bias, d_group, d_output, d_gain_two, d_gate, d_up, d_down)
        return (tuple((left + right for left, right in zip(totals, grads))), (result, grad_in))
    zero_init = (jnp.zeros((D,), jnp.float32), jnp.zeros((D, H * DK), jnp.float32), jnp.zeros((D, H * DK), jnp.float32), jnp.zeros((D, H * DV), jnp.float32), jnp.zeros((D, H * DV), jnp.float32), jnp.zeros((D, R), jnp.float32), jnp.zeros((R, H * DK), jnp.float32), jnp.zeros((H * DK,), jnp.float32), jnp.zeros((DV,), jnp.float32), jnp.zeros((H * DV, D), jnp.float32), jnp.zeros((D,), jnp.float32), jnp.zeros((D, FF), jnp.float32), jnp.zeros((D, FF), jnp.float32), jnp.zeros((FF, D), jnp.float32))
    totals, (block_out, grad_input) = lax.scan(one_sequence, zero_init, (x_in, cotangent))
    return (block_out, grad_input, totals[0], totals[1], totals[2], totals[3], totals[4], totals[5], totals[6], totals[7], totals[8], totals[9], totals[10], totals[11], totals[12], totals[13])
```

```python
import jax
import jax.numpy as jnp
from jax import lax
from jax.experimental import pallas as pl
from jax.experimental.pallas import tpu as pltpu
from jax.sharding import PartitionSpec as P

DK = 128
DV = 256
SPAN = 64


epsilon = 1e-06
normalizer = 16.0
highest = lax.Precision.HIGHEST


def exchange(items, cid):
    axes = []
    for kind, axis, _ in items:
        for name in axis if kind == "wg" else (axis,):
            if name not in axes:
                axes.append(name)
    size = {name: lax.axis_size(name) for name in axes}
    out_shape, scratch = [], []
    for kind, axis, arr in items:
        if kind == "ag":
            out_shape.append(jax.ShapeDtypeStruct((size[axis],) + arr.shape, arr.dtype))
        elif kind == "wg":
            out_shape.append(jax.ShapeDtypeStruct((size[axis[0]],) + arr.shape, arr.dtype))
        else:
            out_shape.append(jax.ShapeDtypeStruct(arr.shape, arr.dtype))
        n = size[axis[0]] if kind == "wg" else size[axis]
        scratch.append(pltpu.SemaphoreType.DMA((2, n)))
        if kind == "ar":
            scratch.append(pltpu.SemaphoreType.DMA((2, n)))
            scratch.append(pltpu.VMEM(arr.shape, arr.dtype))
        elif kind == "wg":
            scratch.append(pltpu.SemaphoreType.DMA((2, n, size[axis[1]])))
        if kind != "ar":
            scratch.append(pltpu.SemaphoreType.DMA)

    def kernel(*refs):
        count = len(items)
        ins, outs, rest = refs[:count], refs[count : 2 * count], list(refs[2 * count :])
        me = {name: lax.axis_index(name) for name in axes}
        barrier = pltpu.get_barrier_semaphore()
        for name in axes:
            for k in range(1, size[name]):
                peer = lax.rem(me[name] + k, size[name])
                pl.semaphore_signal(
                    barrier, inc=1, device_id={name: peer}, device_id_type=pl.DeviceIdType.MESH
                )
        pl.semaphore_wait(barrier, sum(size[name] - 1 for name in axes))

        def remote(source, target, sems, k, name, peer):
            return pltpu.make_async_remote_copy(
                src_ref=source,
                dst_ref=target,
                send_sem=sems.at[(0,) + k],
                recv_sem=sems.at[(1,) + k],
                device_id={name: peer},
                device_id_type=pl.DeviceIdType.MESH,
            )

        waits, later = [], []
        for (kind, axis, arr), src, dst in zip(items, ins, outs):
            sems = rest.pop(0)
            name = axis[0] if kind == "wg" else axis
            n, here = size[name], me[name]
            if kind == "ar":
                sems_two, land = rest.pop(0), rest.pop(0)
                sent = []
                for k in range(1, n):
                    peer = lax.rem(here + k, n)
                    came = lax.rem(here + n - k, n)
                    copy = remote(src.at[peer], land.at[here], sems, (k,), name, peer)
                    copy.start()
                    sent.append((copy, remote(land.at[came], land.at[came], sems, (k,), name, peer)))
                later.append(("ar", src, dst, land, sems_two, name, n, here, sent))
                continue
            if kind == "wg":
                sems_two = rest.pop(0)
            local = rest.pop(0)
            if kind == "wg":
                other = axis[1]
                part = arr.shape[0] // size[other]
                rows = pl.ds(pl.multiple_of(me[other] * part, part), part)
                own = pltpu.make_async_copy(src, dst.at[here], local)
                own.start()
                waits.append(own.wait)
                sent = []
                for k in range(1, n):
                    peer = lax.rem(here + k, n)
                    came = lax.rem(here + n - k, n)
                    copy = remote(src.at[rows], dst.at[here, rows], sems, (k,), name, peer)
                    copy.start()
                    arrived = dst.at[came, rows]
                    sent.append((copy, remote(arrived, arrived, sems, (k,), name, peer), came))
                later.append(("wg", dst, sems_two, other, part, rows, sent))
                continue
            piece = src if kind == "ag" else src.at[here]
            own = pltpu.make_async_copy(piece, dst.at[here], local)
            own.start()
            waits.append(own.wait)
            for k in range(1, n):
                peer = lax.rem(here + k, n)
                came = lax.rem(here + n - k, n)
                piece = src if kind == "ag" else src.at[peer]
                copy = remote(piece, dst.at[here], sems, (k,), name, peer)
                copy.start()
                waits.append(copy.wait_send)
                waits.append(remote(dst.at[came], dst.at[came], sems, (k,), name, peer).wait_recv)
        for entry in later:
            if entry[0] == "ar":
                _, src, dst, land, sems_two, name, n, here, sent = entry
                total = src[here].astype(jnp.float32)
                for k, (copy, arrival) in enumerate(sent, 1):
                    arrival.wait_recv()
                    came = lax.rem(here + n - k, n)
                    total = total + land[came].astype(jnp.float32)
                dst[here] = total.astype(dst.dtype)
                for k in range(1, n):
                    peer = lax.rem(here + k, n)
                    came = lax.rem(here + n - k, n)
                    copy = remote(dst.at[here], dst.at[here], sems_two, (k,), name, peer)
                    copy.start()
                    waits.append(copy.wait_send)
                    waits.append(
                        remote(dst.at[came], dst.at[came], sems_two, (k,), name, peer).wait_recv
                    )
                for copy, _ in sent:
                    waits.append(copy.wait_send)
            else:
                _, dst, sems_two, other, part, rows, sent = entry
                m, place = size[other], me[other]
                for k, (copy, arrival, came) in enumerate(sent, 1):
                    arrival.wait_recv()
                    waits.append(copy.wait_send)
                    for j in range(1, m):
                        partner = lax.rem(place + j, m)
                        whose = lax.rem(place + m - j, m)
                        theirs = dst.at[came, pl.ds(pl.multiple_of(whose * part, part), part)]
                        piece = dst.at[came, rows]
                        onward = remote(piece, piece, sems_two, (k, j), other, partner)
                        onward.start()
                        waits.append(onward.wait_send)
                        waits.append(
                            remote(theirs, theirs, sems_two, (k, j), other, partner).wait_recv
                        )
        for wait in waits:
            wait()

    vmem = pl.BlockSpec(memory_space=pltpu.VMEM)
    return pl.pallas_call(
        kernel,
        out_shape=out_shape,
        in_specs=[vmem] * len(items),
        out_specs=[vmem] * len(items),
        scratch_shapes=scratch,
        compiler_params=pltpu.CompilerParams(
            collective_id=cid, has_side_effects=True, vmem_limit_bytes=60 * 1024 * 1024
        ),
    )(*[item[2] for item in items])


def dot_t(left, right):
    return lax.dot_general(
        left, right, (((1,), (1,)), ((), ())), preferred_element_type=jnp.float32
    )


def dot_rows(left, right):
    return lax.dot_general(
        left, right, (((0,), (0,)), ((), ())), preferred_element_type=jnp.float32
    )


def product(left, right):
    return jnp.dot(left, right, preferred_element_type=jnp.float32)


def rms_rows(inputs):
    return lax.rsqrt(jnp.mean(inputs * inputs, axis=-1, keepdims=True) + epsilon)


def norm_back(inputs, scale, gain, grad):
    scaled = gain * grad
    gain_terms = grad * inputs * scale
    input_grad = scale * scaled - inputs * scale**3 * jnp.mean(
        scaled * inputs, axis=-1, keepdims=True
    )
    return (gain_terms, input_grad)


def mixer_block(queries, keys_in, values_in, log_decay, start_state):
    block_len = min(SPAN, queries.shape[0])
    blocks = queries.shape[0] // block_len

    def cut(array):
        return array.reshape(blocks, block_len, array.shape[-1])

    lower = jnp.tril(jnp.ones((block_len, block_len), jnp.float32))

    def block_step(carried, pieces):
        query_blk, key_blk, value_blk, decay_blk = pieces
        running = jnp.cumsum(decay_blk, axis=0)
        from_state = jnp.dot(query_blk * jnp.exp(running), carried, precision=highest)
        spread = (
            jnp.exp(jnp.minimum(running[:, None, :] - running[None, :, :], 0.0)) * lower[:, :, None]
        )
        scores = jnp.einsum("id,jd,ijd->ij", query_blk, key_blk, spread, precision=highest)
        inside = jnp.dot(scores, value_blk, precision=highest)
        ending = running[-1]
        weighted = key_blk * jnp.exp(ending[None, :] - running)
        carried = jnp.exp(ending)[:, None] * carried + jnp.dot(
            weighted.T, value_blk, precision=highest
        )
        return (carried, from_state + inside)

    final_state, outputs = lax.scan(
        jax.checkpoint(block_step),
        start_state,
        (cut(queries), cut(keys_in), cut(values_in), cut(log_decay)),
    )
    return (outputs.reshape(queries.shape[0], values_in.shape[-1]), final_state)


def on_device(
    x_in,
    cotangent,
    attn_gain,
    w_query,
    w_key,
    w_value,
    w_outgate,
    w_lowrank,
    w_forget,
    forget_bias,
    group_gain,
    w_output,
    mlp_gain,
    w_gate,
    w_up,
    w_down,
):
    seqs_here, tok_here, width = x_in.shape
    total_rows = seqs_here * tok_here
    bf16, f32 = jnp.bfloat16, jnp.float32
    n_seq, n_head, n_dp = lax.axis_size("seq"), lax.axis_size("head"), lax.axis_size("dp")
    seq_pos, head_pos, dp_pos = (
        lax.axis_index("seq"),
        lax.axis_index("head"),
        lax.axis_index("dp"),
    )
    shard_rows = w_query.shape[0]
    part_rows = shard_rows // n_dp
    key_cols, val_cols, hidden = w_query.shape[1], w_value.shape[1], w_gate.shape[1]
    rank = w_lowrank.shape[1]
    heads_here = key_cols // DK
    head_scale = DK ** (-0.5)
    side = -(-(rank + 2) // 128) * 128
    packed = jnp.concatenate(
        (
            w_query,
            w_key,
            w_value,
            w_outgate,
            w_lowrank,
            attn_gain[:, None],
            mlp_gain[:, None],
            jnp.zeros((shard_rows, side - rank - 2), bf16),
            w_output.T,
            w_gate,
            w_up,
            w_down.T,
        ),
        axis=1,
    )
    (weights,) = exchange([("wg", ("seq", "dp"), packed)], 0)
    weights = weights.reshape(width, -1)
    attn_cols = 2 * key_cols + 2 * val_cols
    w_attn = weights[:, :attn_cols]
    w_low = weights[:, attn_cols : attn_cols + side]
    wl_full = w_low[:, :rank]
    gain_first = w_low[:, rank].astype(f32)
    gain_second = w_low[:, rank + 1].astype(f32)
    at = attn_cols + side
    wo_t = weights[:, at : at + val_cols]
    at = at + val_cols
    w_gu = weights[:, at : at + 2 * hidden]
    wdown_t = weights[:, at + 2 * hidden :]
    forget_cols = lax.dynamic_slice_in_dim(w_forget, head_pos * key_cols, key_cols, 1)
    bias_cols = lax.dynamic_slice_in_dim(forget_bias, head_pos * key_cols, key_cols, 0)

    def heads_of(array, size):
        return array.reshape(seqs_here, tok_here, heads_here, size).transpose(0, 2, 1, 3)

    def rows_of(array):
        return array.transpose(0, 2, 1, 3).reshape(total_rows, -1)

    def spread_head(array):
        return array.astype(bf16).reshape(n_head, array.shape[0] // n_head, array.shape[1])

    flat_in = x_in.reshape(total_rows, width)
    flat_cot = cotangent.reshape(total_rows, width)
    scale_one = rms_rows(flat_in)
    normed_in = (flat_in * scale_one * gain_first).astype(bf16)
    proj = product(normed_in, w_attn)
    q_rows = proj[:, :key_cols]
    k_rows = proj[:, key_cols : 2 * key_cols]
    v_rows = proj[:, 2 * key_cols : 2 * key_cols + val_cols]
    og_rows = proj[:, 2 * key_cols + val_cols :]
    low_rank = product(normed_in, wl_full)
    pre_gate = jnp.dot(low_rank, forget_cols, precision=highest) + bias_cols
    log_decay = jax.nn.log_sigmoid(pre_gate) / normalizer
    q_heads = heads_of(q_rows, DK)
    k_heads = heads_of(k_rows, DK)
    v_heads = heads_of(v_rows, DV)
    decay_heads = heads_of(log_decay, DK)
    running = jnp.cumsum(decay_heads, axis=2)
    ending = running[:, :, -1, :]
    decay_total = jnp.exp(ending)
    local_state = jnp.einsum(
        "shld,shlv->shdv",
        k_heads * jnp.exp(ending[:, :, None, :] - running),
        v_heads,
        precision=highest,
    )
    state_shape = local_state.shape
    states, decays = exchange(
        [
            ("ag", "seq", local_state.astype(bf16).reshape(-1, DV)),
            ("ag", "seq", jnp.broadcast_to(decay_total.reshape(1, -1), (8, decay_total.size))),
        ],
        1,
    )
    decays = decays[:, 0].reshape((n_seq,) + decay_total.shape)
    states = states.reshape((n_seq,) + state_shape)
    start_state = jnp.zeros(state_shape, f32)
    for j in range(n_seq - 1):
        start_state = jnp.where(
            j < seq_pos, decays[j][..., None] * start_state + states[j].astype(f32), start_state
        )

    def mixed(q_part, k_part, v_part, d_part):
        return jax.vmap(jax.vmap(mixer_block))(
            q_part * head_scale, k_part, v_part, d_part, start_state
        )

    (o_heads, end_state), pullback = jax.vjp(mixed, q_heads, k_heads, v_heads, decay_heads)
    gate_heads = heads_of(og_rows, DV)
    scale_three = rms_rows(o_heads)
    gated_norm = o_heads * scale_three * group_gain
    gate_sig = jax.nn.sigmoid(gate_heads)
    gate_act = gate_heads * gate_sig
    mixed_out = rows_of(gated_norm * gate_act).astype(bf16)
    (mix_sum,) = exchange([("ar", "head", spread_head(dot_t(mixed_out, wo_t)))], 2)
    resid = flat_in + mix_sum.reshape(total_rows, width).astype(f32)
    scale_two = rms_rows(resid)
    normed_mid = (resid * scale_two * gain_second).astype(bf16)
    both = product(normed_mid, w_gu)
    gate_pre, up_pre = both[:, :hidden], both[:, hidden:]
    gate_sigma = jax.nn.sigmoid(gate_pre)
    gate_silu = gate_pre * gate_sigma
    mlp_hidden = (gate_silu * up_pre).astype(bf16)
    grad_out_b = flat_cot.astype(bf16)
    d_hidden = product(grad_out_b, wdown_t)
    d_gate_pre = (d_hidden * up_pre * gate_sigma * (1.0 + gate_pre * (1.0 - gate_sigma))).astype(
        bf16
    )
    d_up_pre = (d_hidden * gate_silu).astype(bf16)
    d_both = jnp.concatenate((d_gate_pre, d_up_pre), axis=1)
    sums, mid_two, out_two, both_two, hidden_two = exchange(
        [
            (
                "ar",
                "head",
                spread_head(
                    jnp.concatenate((dot_t(mlp_hidden, wdown_t), dot_t(d_both, w_gu)), axis=0)
                ),
            ),
            ("ag", "dp", normed_mid),
            ("ag", "dp", grad_out_b),
            ("ag", "dp", d_both),
            ("ag", "dp", mlp_hidden),
        ],
        3,
    )
    sums = sums.reshape(2, total_rows, width).astype(f32)
    result = resid + sums[0]
    d_normed_mid = sums[1]
    gain_terms, d_resid_norm = norm_back(resid, scale_two, gain_second, d_normed_mid)
    d_gain_two = jnp.sum(gain_terms, axis=0)
    d_resid = flat_cot + d_resid_norm
    d_resid_b = d_resid.astype(bf16)
    d_mixed = heads_of(product(d_resid_b, wo_t), DV)
    d_norm_out = d_mixed * gate_act
    d_gate_heads = d_mixed * gated_norm * gate_sig * (1.0 + gate_heads * (1.0 - gate_sig))
    d_group = jnp.sum(d_norm_out * o_heads * scale_three, axis=(0, 1, 2))
    group_terms, d_o_heads = norm_back(o_heads, scale_three, group_gain, d_norm_out)
    state_grad = jnp.einsum(
        "shld,shlv->shdv", q_heads * head_scale * jnp.exp(running), d_o_heads, precision=highest
    )
    (grads_in,) = exchange([("ag", "seq", state_grad.astype(bf16).reshape(-1, DV))], 4)
    grads_in = grads_in.reshape((n_seq,) + state_shape)
    later_grad = jnp.zeros(state_shape, f32)
    for j in range(n_seq - 1, 0, -1):
        later_grad = jnp.where(
            j > seq_pos, decays[j][..., None] * later_grad + grads_in[j].astype(f32), later_grad
        )
    d_q, d_k, d_v, d_decay = pullback((d_o_heads, later_grad))
    d_pre = rows_of(d_decay) / normalizer * jax.nn.sigmoid(-pre_gate)
    d_bias = jnp.sum(d_pre, axis=0)
    d_forget = jnp.dot(low_rank.T, d_pre, precision=highest)
    d_low_part = jnp.dot(d_pre, forget_cols.T, precision=highest)
    d_proj = jnp.concatenate(
        (
            rows_of(d_q).astype(bf16),
            rows_of(d_k).astype(bf16),
            rows_of(d_v).astype(bf16),
            rows_of(d_gate_heads).astype(bf16),
        ),
        axis=1,
    )
    d_in_part = jnp.concatenate(
        (dot_t(d_proj, w_attn), d_low_part, jnp.zeros((total_rows, side - rank), f32)), axis=1
    )
    group_rows = d_group.reshape(1, DV)
    if DV < key_cols:
        group_rows = jnp.pad(group_rows, ((0, 0), (0, key_cols - DV)))
    if DV > key_cols:
        group_rows = group_rows.reshape(-1, key_cols)
    used = rank + 1 + group_rows.shape[0]
    small = jnp.concatenate(
        (
            d_forget,
            d_bias[None, :],
            group_rows,
            jnp.zeros((-used % 8, key_cols), f32),
        ),
        axis=0,
    )
    in_sum, small_seq, in_two, proj_two, mixed_two, resid_two = exchange(
        [
            ("ar", "head", spread_head(d_in_part)),
            ("ag", "seq", small),
            ("ag", "dp", normed_in),
            ("ag", "dp", d_proj),
            ("ag", "dp", mixed_out),
            ("ag", "dp", d_resid_b),
        ],
        5,
    )
    in_sum = in_sum.reshape(total_rows, width + side)
    d_low_b = in_sum[:, width : width + rank]
    d_normed_in = in_sum[:, :width].astype(f32) + dot_t(d_low_b, wl_full)
    first_terms, d_in_norm = norm_back(flat_in, scale_one, gain_first, d_normed_in)
    d_gain_one = jnp.sum(first_terms, axis=0)
    grad_in = d_resid + d_in_norm

    def my_rows(array):
        array = array.reshape(n_dp * total_rows, n_seq, n_dp, part_rows)
        array = lax.dynamic_index_in_dim(array, dp_pos, 2, False)
        return array.reshape(n_dp * total_rows, n_seq * part_rows)

    def all_rows(array):
        return array.reshape(n_dp * total_rows, -1)

    grads = jnp.concatenate(
        (
            dot_rows(my_rows(in_two), all_rows(proj_two)).astype(bf16),
            dot_rows(my_rows(resid_two), all_rows(mixed_two)).astype(bf16),
            dot_rows(my_rows(mid_two), all_rows(both_two)).astype(bf16),
            dot_rows(my_rows(out_two), all_rows(hidden_two)).astype(bf16),
        ),
        axis=1,
    ).reshape(n_seq, part_rows, -1)
    tall = jnp.concatenate(
        (
            dot_rows(d_low_b, normed_in),
            d_gain_one[None, :],
            d_gain_two[None, :],
            jnp.zeros((-(rank + 2) % 8, width), f32),
        ),
        axis=0,
    )
    tall = tall.reshape(-1, n_seq, shard_rows).transpose(1, 0, 2)
    grads, tall, small = exchange(
        [
            ("a2a", "seq", grads),
            ("a2a", "seq", tall),
            ("ag", "head", jnp.sum(small_seq, axis=0)),
        ],
        6,
    )
    grads, tall, small = exchange(
        [
            ("ag", "dp", jnp.sum(grads.astype(f32), axis=0)),
            ("ag", "dp", jnp.sum(tall, axis=0)),
            ("ag", "dp", small.reshape(-1, key_cols)),
        ],
        7,
    )
    grads = grads.reshape(shard_rows, -1)
    tall = jnp.sum(tall, axis=0)
    small = jnp.sum(small, axis=0).reshape(n_head, -1, key_cols)
    s_forget = small[:, :rank].transpose(1, 0, 2).reshape(rank, -1)
    s_bias = small[:, rank].reshape(-1)
    s_group = jnp.sum(small[:, rank + 1 : used], axis=0).reshape(-1)[:DV]
    cuts = [key_cols, 2 * key_cols, 2 * key_cols + val_cols, attn_cols, attn_cols + val_cols]
    cuts = cuts + [cuts[-1] + hidden, cuts[-1] + 2 * hidden]
    s_query, s_key, s_value, s_outgate, s_output, s_gate, s_up, s_down = jnp.split(
        grads, cuts, axis=1
    )
    return (
        result.reshape(seqs_here, tok_here, width),
        grad_in.reshape(seqs_here, tok_here, width),
        tall[rank],
        s_query,
        s_key,
        s_value,
        s_outgate,
        tall[:rank].T,
        s_forget,
        s_bias,
        s_group,
        s_output.T,
        tall[rank + 1],
        s_gate,
        s_up,
        s_down.T,
    )


def solution(mesh):
    return jax.shard_map(
        on_device,
        mesh=mesh,
        in_specs=(
            P("dp", "seq", None),
            P("dp", "seq", None),
            P("seq"),
            P("seq", "head"),
            P("seq", "head"),
            P("seq", "head"),
            P("seq", "head"),
            P("seq", None),
            P(),
            P(),
            P(),
            P("head", "seq"),
            P("seq"),
            P("seq", "head"),
            P("seq", "head"),
            P("head", "seq"),
        ),
        out_specs=(
            P("dp", "seq", None),
            P("dp", "seq", None),
            P("seq"),
            P("seq", "head"),
            P("seq", "head"),
            P("seq", "head"),
            P("seq", "head"),
            P("seq", None),
            P(),
            P(),
            P(),
            P("head", "seq"),
            P("seq"),
            P("seq", "head"),
            P("seq", "head"),
            P("head", "seq"),
        ),
        check_vma=False,
    )
```

```python
import jax
import jax.numpy as jnp
from jax import lax
from jax.experimental import pallas as pl
from jax.experimental.pallas import tpu as pltpu
from jax.sharding import PartitionSpec as P

DK = 128
DV = 256
SPAN = 64


epsilon = 1e-06
normalizer = 16.0
highest = lax.Precision.HIGHEST


def exchange(items, cid):
    groups = []
    for kind, axis, _ in items:
        for name in axis if kind in ("wg", "rs") else (axis,):
            if name not in groups:
                groups.append(name)
    names = []
    for group in groups:
        for name in group if isinstance(group, tuple) else (group,):
            if name not in names:
                names.append(name)
    size = {name: lax.axis_size(name) for name in names}
    for group in groups:
        if isinstance(group, tuple):
            size[group] = size[group[0]] * size[group[1]]
    out_shape, scratch = [], []
    dma = pltpu.SemaphoreType.DMA
    for kind, axis, arr in items:
        if kind in ("wg", "rs"):
            n, m = size[axis[0]], size[axis[1]]
            scratch += [dma((2, 2, n)), dma((2, 2, n, m))]
            if kind == "wg":
                out_shape.append(jax.ShapeDtypeStruct((n,) + arr.shape, arr.dtype))
                scratch.append(dma)
            else:
                out_shape.append(jax.ShapeDtypeStruct((m,) + arr.shape[1:], jnp.float32))
                scratch.append(pltpu.VMEM((2,) + arr.shape, arr.dtype))
                scratch.append(pltpu.VMEM((2,) + arr.shape, arr.dtype))
            continue
        n = size[axis]
        scratch.append(dma((2, n)))
        if kind == "ar":
            out_shape.append(jax.ShapeDtypeStruct(arr.shape, arr.dtype))
            scratch += [dma((2, n)), pltpu.VMEM(arr.shape, arr.dtype)]
        else:
            inner = arr.shape if kind == "ag" else arr.shape[1:]
            out_shape.append(jax.ShapeDtypeStruct((n,) + inner, arr.dtype))
            scratch.append(dma)

    def kernel(*refs):
        count = len(items)
        ins, outs, rest = refs[:count], refs[count : 2 * count], list(refs[2 * count :])
        me = {name: lax.axis_index(name) for name in names}
        for group in groups:
            if isinstance(group, tuple):
                me[group] = me[group[0]] * size[group[1]] + me[group[1]]

        def device(group, place):
            if isinstance(group, tuple):
                return {
                    group[0]: place // size[group[1]],
                    group[1]: lax.rem(place, size[group[1]]),
                }
            return {group: place}

        barrier = pltpu.get_barrier_semaphore()
        for group in groups:
            for k in range(1, size[group]):
                pl.semaphore_signal(
                    barrier,
                    inc=1,
                    device_id=device(group, lax.rem(me[group] + k, size[group])),
                    device_id_type=pl.DeviceIdType.MESH,
                )
        pl.semaphore_wait(barrier, sum(size[group] - 1 for group in groups))

        def remote(source, target, send, recv, group, place):
            return pltpu.make_async_remote_copy(
                src_ref=source,
                dst_ref=target,
                send_sem=send,
                recv_sem=recv,
                device_id=device(group, place),
                device_id_type=pl.DeviceIdType.MESH,
            )

        waits, chains, sums = [], [], []

        def chain_gather(src, dst, sems, sems_two, local, axis, arr):
            name, other = axis
            n, here, m, place = size[name], me[name], size[other], me[other]
            part = arr.shape[0] // m
            rows = pl.ds(pl.multiple_of(place * part, part), part)
            own = pltpu.make_async_copy(src, dst.at[here], local)
            own.start()
            waits.append(own.wait)

            def hop(way, step, source, index):
                to = here + 1 if way == 0 else here - 1
                return remote(
                    source,
                    dst.at[index, rows],
                    sems.at[way, 0, step],
                    sems.at[way, 1, step],
                    name,
                    to,
                )

            def guarded(ok, call):
                waits.append(lambda: pl.when(ok)(call))

            open_ends = (here < n - 1, here > 0)
            for way in range(2):
                @pl.when(open_ends[way])
                def _():
                    hop(way, 0, src.at[rows], here).start()

                guarded(
                    open_ends[way],
                    lambda way=way: hop(way, 0, src.at[rows], here).wait_send(),
                )

            def advance(step):
                for way in range(2):
                    came = here - 1 - step if way == 0 else here + 1 + step
                    ok = came >= 0 if way == 0 else came < n
                    on = jnp.logical_and(ok, open_ends[way])

                    def partners(way=way, came=came):
                        for j in range(1, m):
                            to = lax.rem(place + j, m)
                            whose = lax.rem(place + m - j, m)
                            piece = dst.at[came, rows]
                            theirs = dst.at[came, pl.ds(pl.multiple_of(whose * part, part), part)]
                            send, recv = sems_two.at[way, 0, step, j], sems_two.at[way, 1, step, j]
                            yield (
                                remote(piece, piece, send, recv, other, to),
                                remote(theirs, theirs, send, recv, other, to),
                            )

                    @pl.when(ok)
                    def _():
                        hop(way, step, dst.at[came, rows], came).wait_recv()

                    if step + 1 < n - 1:
                        @pl.when(on)
                        def _():
                            hop(way, step + 1, dst.at[came, rows], came).start()

                        guarded(
                            on,
                            lambda way=way, came=came: hop(
                                way, step + 1, dst.at[came, rows], came
                            ).wait_send(),
                        )

                    @pl.when(ok)
                    def _():
                        for copy, _ in partners():
                            copy.start()

                    def finish(partners=partners):
                        for copy, arrival in partners():
                            copy.wait_send()
                            arrival.wait_recv()

                    guarded(ok, finish)

            chains.append((n - 1, advance, lambda: None))

        def chain_sum(src, dst, sems, sems_two, land, held, axis, arr):
            name, other = axis
            n, here, m, place = size[name], me[name], size[other], me[other]
            tall = 16 if arr.shape[1] % 16 == 0 else arr.shape[1]
            turns = arr.shape[1] // tall

            def by_rows(call):
                def one(turn, carry):
                    call(pl.ds(pl.multiple_of(turn * tall, tall), tall))
                    return carry

                lax.fori_loop(0, turns, one, 0)

            def hop(way, step, source, index):
                to = here + 1 if way == 0 else here - 1
                return remote(
                    source,
                    land.at[way, index],
                    sems.at[way, 0, step],
                    sems.at[way, 1, step],
                    name,
                    to,
                )

            def guarded(ok, call):
                waits.append(lambda: pl.when(ok)(call))

            firsts = (here == 0, here == n - 1)

            def advance(step):
                for way in range(2):
                    goal = n - 1 - step if way == 0 else step
                    passing = here < goal if way == 0 else here > goal
                    inner = jnp.logical_and(passing, jnp.logical_not(firsts[way]))
                    first = jnp.logical_and(passing, firsts[way])

                    @pl.when(first)
                    def _():
                        hop(way, step, src.at[goal], goal).start()

                    guarded(
                        first,
                        lambda way=way, goal=goal: hop(way, step, src.at[goal], goal).wait_send(),
                    )

                    @pl.when(inner)
                    def _():
                        hop(way, step, land.at[way, goal], goal).wait_recv()

                        def add(rows):
                            held[way, goal, rows] = (
                                land[way, goal, rows].astype(jnp.float32)
                                + src[goal, rows].astype(jnp.float32)
                            ).astype(held.dtype)

                        by_rows(add)
                        hop(way, step, held.at[way, goal], goal).start()

                    guarded(
                        inner,
                        lambda way=way, goal=goal: hop(
                            way, step, held.at[way, goal], goal
                        ).wait_send(),
                    )

            def partners():
                for j in range(1, m):
                    to = lax.rem(place + j, m)
                    whose = lax.rem(place + m - j, m)
                    send, recv = sems_two.at[0, 0, 0, j], sems_two.at[0, 1, 0, j]
                    yield (
                        remote(dst.at[place], dst.at[place], send, recv, other, to),
                        remote(dst.at[whose], dst.at[whose], send, recv, other, to),
                    )

            def close():
                def start(rows):
                    dst[place, rows] = src[here, rows].astype(jnp.float32)

                by_rows(start)
                for way in range(2):
                    step = n - 1 - here if way == 0 else here

                    @pl.when(jnp.logical_not(firsts[way]))
                    def _():
                        hop(way, step, land.at[way, here], here).wait_recv()

                        def add(rows):
                            dst[place, rows] = dst[place, rows] + land[way, here, rows].astype(
                                jnp.float32
                            )

                        by_rows(add)

                for copy, _ in partners():
                    copy.start()
                for copy, arrival in partners():
                    waits.append(copy.wait_send)
                    waits.append(arrival.wait_recv)

            chains.append((n, advance, close))

        for (kind, axis, arr), src, dst in zip(items, ins, outs):
            if kind in ("wg", "rs"):
                extra = [rest.pop(0) for _ in range(3 if kind == "wg" else 4)]
                (chain_gather if kind == "wg" else chain_sum)(src, dst, *extra, axis, arr)
                continue
            sems = rest.pop(0)
            n, here = size[axis], me[axis]
            if kind == "ar":
                sems_two, land = rest.pop(0), rest.pop(0)
                sent = []
                for k in range(1, n):
                    peer = lax.rem(here + k, n)
                    came = lax.rem(here + n - k, n)
                    pair = sems.at[0, k], sems.at[1, k]
                    copy = remote(src.at[peer], land.at[here], *pair, axis, peer)
                    copy.start()
                    sent.append((copy, remote(land.at[came], land.at[came], *pair, axis, peer)))
                sums.append((src, dst, land, sems_two, axis, n, here, sent))
                continue
            local = rest.pop(0)

            def piece(place):
                if kind == "ag":
                    return src
                if isinstance(axis, tuple):
                    return src.at[place // size[axis[1]]]
                return src.at[place]

            own = pltpu.make_async_copy(piece(here), dst.at[here], local)
            own.start()
            waits.append(own.wait)
            for k in range(1, n):
                peer = lax.rem(here + k, n)
                came = lax.rem(here + n - k, n)
                pair = sems.at[0, k], sems.at[1, k]
                copy = remote(piece(peer), dst.at[here], *pair, axis, peer)
                copy.start()
                waits.append(copy.wait_send)
                waits.append(remote(dst.at[came], dst.at[came], *pair, axis, peer).wait_recv)

        def finish_sums():
            for src, dst, land, sems_two, axis, n, here, sent in sums:
                total = src[here].astype(jnp.float32)
                for k, (copy, arrival) in enumerate(sent, 1):
                    arrival.wait_recv()
                    total = total + land[lax.rem(here + n - k, n)].astype(jnp.float32)
                dst[here] = total.astype(dst.dtype)
                for k in range(1, n):
                    peer = lax.rem(here + k, n)
                    came = lax.rem(here + n - k, n)
                    pair = sems_two.at[0, k], sems_two.at[1, k]
                    copy = remote(dst.at[here], dst.at[here], *pair, axis, peer)
                    copy.start()
                    waits.append(copy.wait_send)
                    waits.append(
                        remote(dst.at[came], dst.at[came], *pair, axis, peer).wait_recv
                    )
                for copy, _ in sent:
                    waits.append(copy.wait_send)

        steps = max([entry[0] for entry in chains], default=0)
        for step in range(steps):
            if step == 1:
                finish_sums()
            for last, advance, _ in chains:
                if step < last:
                    advance(step)
        if steps < 2:
            finish_sums()
        for _, _, close in chains:
            close()
        for wait in waits:
            wait()

    vmem = pl.BlockSpec(memory_space=pltpu.VMEM)
    return pl.pallas_call(
        kernel,
        out_shape=out_shape,
        in_specs=[vmem] * len(items),
        out_specs=[vmem] * len(items),
        scratch_shapes=scratch,
        compiler_params=pltpu.CompilerParams(
            collective_id=cid, has_side_effects=True, vmem_limit_bytes=60 * 1024 * 1024
        ),
    )(*[item[2] for item in items])


def dot_t(left, right):
    return lax.dot_general(
        left, right, (((1,), (1,)), ((), ())), preferred_element_type=jnp.float32
    )


def dot_rows(left, right):
    return lax.dot_general(
        left, right, (((0,), (0,)), ((), ())), preferred_element_type=jnp.float32
    )


def product(left, right):
    return jnp.dot(left, right, preferred_element_type=jnp.float32)


def rms_rows(inputs):
    return lax.rsqrt(jnp.mean(inputs * inputs, axis=-1, keepdims=True) + epsilon)


def norm_back(inputs, scale, gain, grad):
    scaled = gain * grad
    gain_terms = grad * inputs * scale
    input_grad = scale * scaled - inputs * scale**3 * jnp.mean(
        scaled * inputs, axis=-1, keepdims=True
    )
    return (gain_terms, input_grad)


def mixer_block(queries, keys_in, values_in, log_decay, start_state):
    block_len = min(SPAN, queries.shape[0])
    blocks = queries.shape[0] // block_len

    def cut(array):
        return array.reshape(blocks, block_len, array.shape[-1])

    lower = jnp.tril(jnp.ones((block_len, block_len), jnp.float32))

    def block_step(carried, pieces):
        query_blk, key_blk, value_blk, decay_blk = pieces
        running = jnp.cumsum(decay_blk, axis=0)
        from_state = jnp.dot(query_blk * jnp.exp(running), carried, precision=highest)
        spread = (
            jnp.exp(jnp.minimum(running[:, None, :] - running[None, :, :], 0.0)) * lower[:, :, None]
        )
        scores = jnp.einsum("id,jd,ijd->ij", query_blk, key_blk, spread, precision=highest)
        inside = jnp.dot(scores, value_blk, precision=highest)
        ending = running[-1]
        weighted = key_blk * jnp.exp(ending[None, :] - running)
        carried = jnp.exp(ending)[:, None] * carried + jnp.dot(
            weighted.T, value_blk, precision=highest
        )
        return (carried, from_state + inside)

    final_state, outputs = lax.scan(
        jax.checkpoint(block_step),
        start_state,
        (cut(queries), cut(keys_in), cut(values_in), cut(log_decay)),
    )
    return (outputs.reshape(queries.shape[0], values_in.shape[-1]), final_state)


def on_device(
    x_in,
    cotangent,
    attn_gain,
    w_query,
    w_key,
    w_value,
    w_outgate,
    w_lowrank,
    w_forget,
    forget_bias,
    group_gain,
    w_output,
    mlp_gain,
    w_gate,
    w_up,
    w_down,
):
    seqs_here, tok_here, width = x_in.shape
    total_rows = seqs_here * tok_here
    bf16, f32 = jnp.bfloat16, jnp.float32
    n_seq, n_head, n_dp = lax.axis_size("seq"), lax.axis_size("head"), lax.axis_size("dp")
    seq_pos, head_pos = lax.axis_index("seq"), lax.axis_index("head")
    shard_rows = w_query.shape[0]
    part_rows = shard_rows // n_dp
    key_cols, val_cols, hidden = w_query.shape[1], w_value.shape[1], w_gate.shape[1]
    rank = w_lowrank.shape[1]
    heads_here = key_cols // DK
    head_scale = DK ** (-0.5)
    side = -(-(rank + 2) // 128) * 128
    packed = jnp.concatenate(
        (
            w_query,
            w_key,
            w_value,
            w_outgate,
            w_lowrank,
            attn_gain[:, None],
            mlp_gain[:, None],
            jnp.zeros((shard_rows, side - rank - 2), bf16),
            w_output.T,
        ),
        axis=1,
    )
    packed_mlp = jnp.concatenate((w_gate, w_up, w_down.T), axis=1)
    (weights,) = exchange([("wg", ("seq", "dp"), packed)], 0)
    weights = weights.reshape(width, -1)
    attn_cols = 2 * key_cols + 2 * val_cols
    w_attn = weights[:, :attn_cols]
    w_low = weights[:, attn_cols : attn_cols + side]
    wl_full = w_low[:, :rank]
    gain_first = w_low[:, rank].astype(f32)
    gain_second = w_low[:, rank + 1].astype(f32)
    at = attn_cols + side
    wo_t = weights[:, at : at + val_cols]
    forget_cols = lax.dynamic_slice_in_dim(w_forget, head_pos * key_cols, key_cols, 1)
    bias_cols = lax.dynamic_slice_in_dim(forget_bias, head_pos * key_cols, key_cols, 0)

    def heads_of(array, size):
        return array.reshape(seqs_here, tok_here, heads_here, size).transpose(0, 2, 1, 3)

    def rows_of(array):
        return array.transpose(0, 2, 1, 3).reshape(total_rows, -1)

    def spread_head(array):
        return array.astype(bf16).reshape(n_head, array.shape[0] // n_head, array.shape[1])

    def by_part(array):
        array = array.reshape(total_rows, n_seq, n_dp, part_rows)
        return array.transpose(2, 0, 1, 3).reshape(n_dp, total_rows, n_seq * part_rows)

    def all_rows(array):
        return array.reshape(n_dp * total_rows, -1)

    def grad_of(left, right):
        return dot_rows(all_rows(left), all_rows(right)).astype(bf16)

    flat_in = x_in.reshape(total_rows, width)
    flat_cot = cotangent.reshape(total_rows, width)
    scale_one = rms_rows(flat_in)
    normed_in = (flat_in * scale_one * gain_first).astype(bf16)
    proj = product(normed_in, w_attn)
    q_rows = proj[:, :key_cols]
    k_rows = proj[:, key_cols : 2 * key_cols]
    v_rows = proj[:, 2 * key_cols : 2 * key_cols + val_cols]
    og_rows = proj[:, 2 * key_cols + val_cols :]
    low_rank = product(normed_in, wl_full)
    pre_gate = jnp.dot(low_rank, forget_cols, precision=highest) + bias_cols
    log_decay = jax.nn.log_sigmoid(pre_gate) / normalizer
    q_heads = heads_of(q_rows, DK)
    k_heads = heads_of(k_rows, DK)
    v_heads = heads_of(v_rows, DV)
    decay_heads = heads_of(log_decay, DK)
    running = jnp.cumsum(decay_heads, axis=2)
    ending = running[:, :, -1, :]
    decay_total = jnp.exp(ending)
    local_state = jnp.einsum(
        "shld,shlv->shdv",
        k_heads * jnp.exp(ending[:, :, None, :] - running),
        v_heads,
        precision=highest,
    )
    state_shape = local_state.shape
    states, decays = exchange(
        [
            ("ag", "seq", local_state.astype(bf16).reshape(-1, DV)),
            ("ag", "seq", jnp.broadcast_to(decay_total.reshape(1, -1), (8, decay_total.size))),
        ],
        1,
    )
    decays = decays[:, 0].reshape((n_seq,) + decay_total.shape)
    states = states.reshape((n_seq,) + state_shape)
    start_state = jnp.zeros(state_shape, f32)
    for j in range(n_seq - 1):
        start_state = jnp.where(
            j < seq_pos, decays[j][..., None] * start_state + states[j].astype(f32), start_state
        )

    def mixed(q_part, k_part, v_part, d_part):
        return jax.vmap(jax.vmap(mixer_block))(
            q_part * head_scale, k_part, v_part, d_part, start_state
        )

    (o_heads, end_state), pullback = jax.vjp(mixed, q_heads, k_heads, v_heads, decay_heads)
    gate_heads = heads_of(og_rows, DV)
    scale_three = rms_rows(o_heads)
    gated_norm = o_heads * scale_three * group_gain
    gate_sig = jax.nn.sigmoid(gate_heads)
    gate_act = gate_heads * gate_sig
    mixed_out = rows_of(gated_norm * gate_act).astype(bf16)
    mix_sum, weights_mlp = exchange(
        [
            ("ar", "head", spread_head(dot_t(mixed_out, wo_t))),
            ("wg", ("seq", "dp"), packed_mlp),
        ],
        2,
    )
    weights_mlp = weights_mlp.reshape(width, -1)
    w_gu = weights_mlp[:, : 2 * hidden]
    wdown_t = weights_mlp[:, 2 * hidden :]
    resid = flat_in + mix_sum.reshape(total_rows, width).astype(f32)
    scale_two = rms_rows(resid)
    normed_mid = (resid * scale_two * gain_second).astype(bf16)
    both = product(normed_mid, w_gu)
    gate_pre, up_pre = both[:, :hidden], both[:, hidden:]
    gate_sigma = jax.nn.sigmoid(gate_pre)
    gate_silu = gate_pre * gate_sigma
    mlp_hidden = (gate_silu * up_pre).astype(bf16)
    grad_out_b = flat_cot.astype(bf16)
    d_hidden = product(grad_out_b, wdown_t)
    d_gate_pre = (d_hidden * up_pre * gate_sigma * (1.0 + gate_pre * (1.0 - gate_sigma))).astype(
        bf16
    )
    d_up_pre = (d_hidden * gate_silu).astype(bf16)
    d_both = jnp.concatenate((d_gate_pre, d_up_pre), axis=1)
    sums, mid_two, out_two, both_two, hidden_two = exchange(
        [
            (
                "ar",
                "head",
                spread_head(
                    jnp.concatenate((dot_t(mlp_hidden, wdown_t), dot_t(d_both, w_gu)), axis=0)
                ),
            ),
            ("a2a", "dp", by_part(normed_mid)),
            ("a2a", "dp", by_part(grad_out_b)),
            ("ag", "dp", d_both),
            ("ag", "dp", mlp_hidden),
        ],
        3,
    )
    sums = sums.reshape(2, total_rows, width).astype(f32)
    result = resid + sums[0]
    d_normed_mid = sums[1]
    gain_terms, d_resid_norm = norm_back(resid, scale_two, gain_second, d_normed_mid)
    d_gain_two = jnp.sum(gain_terms, axis=0)
    d_resid = flat_cot + d_resid_norm
    d_resid_b = d_resid.astype(bf16)
    d_mixed = heads_of(product(d_resid_b, wo_t), DV)
    d_norm_out = d_mixed * gate_act
    d_gate_heads = d_mixed * gated_norm * gate_sig * (1.0 + gate_heads * (1.0 - gate_sig))
    d_group = jnp.sum(d_norm_out * o_heads * scale_three, axis=(0, 1, 2))
    group_terms, d_o_heads = norm_back(o_heads, scale_three, group_gain, d_norm_out)
    state_grad = jnp.einsum(
        "shld,shlv->shdv", q_heads * head_scale * jnp.exp(running), d_o_heads, precision=highest
    )
    grads_in, mixed_two, resid_two = exchange(
        [
            ("ag", "seq", state_grad.astype(bf16).reshape(-1, DV)),
            ("ag", "dp", mixed_out),
            ("a2a", "dp", by_part(d_resid_b)),
        ],
        4,
    )
    grads_late = jnp.concatenate(
        (
            grad_of(resid_two, mixed_two),
            grad_of(mid_two, both_two),
            grad_of(out_two, hidden_two),
        ),
        axis=1,
    ).reshape(n_seq, part_rows, -1)
    grads_in = grads_in.reshape((n_seq,) + state_shape)
    later_grad = jnp.zeros(state_shape, f32)
    for j in range(n_seq - 1, 0, -1):
        later_grad = jnp.where(
            j > seq_pos, decays[j][..., None] * later_grad + grads_in[j].astype(f32), later_grad
        )
    d_q, d_k, d_v, d_decay = pullback((d_o_heads, later_grad))
    d_pre = rows_of(d_decay) / normalizer * jax.nn.sigmoid(-pre_gate)
    d_bias = jnp.sum(d_pre, axis=0)
    d_forget = jnp.dot(low_rank.T, d_pre, precision=highest)
    d_low_part = jnp.dot(d_pre, forget_cols.T, precision=highest)
    d_proj = jnp.concatenate(
        (
            rows_of(d_q).astype(bf16),
            rows_of(d_k).astype(bf16),
            rows_of(d_v).astype(bf16),
            rows_of(d_gate_heads).astype(bf16),
        ),
        axis=1,
    )
    d_in_part = jnp.concatenate(
        (dot_t(d_proj, w_attn), d_low_part, jnp.zeros((total_rows, side - rank), f32)), axis=1
    )
    group_rows = d_group.reshape(1, DV)
    if DV < key_cols:
        group_rows = jnp.pad(group_rows, ((0, 0), (0, key_cols - DV)))
    if DV > key_cols:
        group_rows = group_rows.reshape(-1, key_cols)
    used = rank + 1 + group_rows.shape[0]
    small = jnp.concatenate(
        (
            d_forget,
            d_bias[None, :],
            group_rows,
            jnp.zeros((-used % 8, key_cols), f32),
        ),
        axis=0,
    )
    grads_late, in_sum, small_all, in_two, proj_two = exchange(
        [
            ("rs", ("seq", "dp"), grads_late),
            ("ar", "head", spread_head(d_in_part)),
            ("ag", ("seq", "dp"), small),
            ("a2a", "dp", by_part(normed_in)),
            ("ag", "dp", d_proj),
        ],
        5,
    )
    in_sum = in_sum.reshape(total_rows, width + side)
    d_low_b = in_sum[:, width : width + rank]
    d_normed_in = in_sum[:, :width].astype(f32) + dot_t(d_low_b, wl_full)
    first_terms, d_in_norm = norm_back(flat_in, scale_one, gain_first, d_normed_in)
    d_gain_one = jnp.sum(first_terms, axis=0)
    grad_in = d_resid + d_in_norm

    grads_attn = grad_of(in_two, proj_two).reshape(n_seq, part_rows, -1)
    tall = jnp.concatenate(
        (
            dot_rows(d_low_b, normed_in),
            d_gain_one[None, :],
            d_gain_two[None, :],
            jnp.zeros((-(rank + 2) % 8, width), f32),
        ),
        axis=0,
    )
    tall = tall.reshape(-1, n_seq, shard_rows).transpose(1, 0, 2)
    grads_attn, tall, small = exchange(
        [
            ("rs", ("seq", "dp"), grads_attn),
            ("a2a", ("seq", "dp"), tall),
            ("ag", "head", jnp.sum(small_all, axis=0)),
        ],
        6,
    )
    grads_attn = grads_attn.reshape(shard_rows, -1)
    grads_late = grads_late.reshape(shard_rows, -1)
    tall = jnp.sum(tall, axis=0)
    s_forget = small[:, :rank].transpose(1, 0, 2).reshape(rank, -1)
    s_bias = small[:, rank].reshape(-1)
    s_group = jnp.sum(small[:, rank + 1 : used], axis=0).reshape(-1)[:DV]
    s_query, s_key, s_value, s_outgate = jnp.split(
        grads_attn, [key_cols, 2 * key_cols, 2 * key_cols + val_cols], axis=1
    )
    s_output, s_gate, s_up, s_down = jnp.split(
        grads_late, [val_cols, val_cols + hidden, val_cols + 2 * hidden], axis=1
    )
    return (
        result.reshape(seqs_here, tok_here, width),
        grad_in.reshape(seqs_here, tok_here, width),
        tall[rank],
        s_query,
        s_key,
        s_value,
        s_outgate,
        tall[:rank].T,
        s_forget,
        s_bias,
        s_group,
        s_output.T,
        tall[rank + 1],
        s_gate,
        s_up,
        s_down.T,
    )


def solution(mesh):
    return jax.shard_map(
        on_device,
        mesh=mesh,
        in_specs=(
            P("dp", "seq", None),
            P("dp", "seq", None),
            P("seq"),
            P("seq", "head"),
            P("seq", "head"),
            P("seq", "head"),
            P("seq", "head"),
            P("seq", None),
            P(),
            P(),
            P(),
            P("head", "seq"),
            P("seq"),
            P("seq", "head"),
            P("seq", "head"),
            P("head", "seq"),
        ),
        out_specs=(
            P("dp", "seq", None),
            P("dp", "seq", None),
            P("seq"),
            P("seq", "head"),
            P("seq", "head"),
            P("seq", "head"),
            P("seq", "head"),
            P("seq", None),
            P(),
            P(),
            P(),
            P("head", "seq"),
            P("seq"),
            P("seq", "head"),
            P("seq", "head"),
            P("head", "seq"),
        ),
        check_vma=False,
    )
```

```python
import jax
import jax.numpy as jnp
from jax import lax
from jax.experimental import pallas as pl
from jax.experimental.pallas import tpu as pltpu
from jax.sharding import PartitionSpec as P

DK = 128
DV = 256
SPAN = 64


epsilon = 1e-06
normalizer = 16.0
highest = lax.Precision.HIGHEST


def exchange(items, cid):
    groups = []
    for kind, axis, _ in items:
        for name in axis if kind in ("wg", "rs") else (axis,):
            if name not in groups:
                groups.append(name)
    names = []
    for group in groups:
        for name in group if isinstance(group, tuple) else (group,):
            if name not in names:
                names.append(name)
    size = {name: lax.axis_size(name) for name in names}
    for group in groups:
        if isinstance(group, tuple):
            size[group] = size[group[0]] * size[group[1]]
    out_shape, scratch = [], []
    dma = pltpu.SemaphoreType.DMA
    for kind, axis, arr in items:
        if kind in ("wg", "rs"):
            n, m = size[axis[0]], size[axis[1]]
            scratch += [dma((2, 2, n)), dma((2, 2, n, m))]
            if kind == "wg":
                out_shape.append(jax.ShapeDtypeStruct((n,) + arr.shape, arr.dtype))
                scratch.append(dma)
            else:
                out_shape.append(jax.ShapeDtypeStruct((m,) + arr.shape[1:], jnp.float32))
                scratch.append(pltpu.VMEM((2,) + arr.shape, arr.dtype))
                scratch.append(pltpu.VMEM((2,) + arr.shape, arr.dtype))
            continue
        n = size[axis]
        scratch.append(dma((2, n)))
        if kind == "ar":
            out_shape.append(jax.ShapeDtypeStruct(arr.shape, arr.dtype))
            scratch += [dma((2, n)), pltpu.VMEM(arr.shape, arr.dtype)]
        else:
            inner = arr.shape if kind == "ag" else arr.shape[1:]
            out_shape.append(jax.ShapeDtypeStruct((n,) + inner, arr.dtype))
            scratch.append(dma)

    def kernel(*refs):
        count = len(items)
        ins, outs, rest = refs[:count], refs[count : 2 * count], list(refs[2 * count :])
        me = {name: lax.axis_index(name) for name in names}
        for group in groups:
            if isinstance(group, tuple):
                me[group] = me[group[0]] * size[group[1]] + me[group[1]]

        def device(group, place):
            if isinstance(group, tuple):
                return {
                    group[0]: place // size[group[1]],
                    group[1]: lax.rem(place, size[group[1]]),
                }
            return {group: place}

        barrier = pltpu.get_barrier_semaphore()
        for group in groups:
            for k in range(1, size[group]):
                pl.semaphore_signal(
                    barrier,
                    inc=1,
                    device_id=device(group, lax.rem(me[group] + k, size[group])),
                    device_id_type=pl.DeviceIdType.MESH,
                )
        pl.semaphore_wait(barrier, sum(size[group] - 1 for group in groups))

        def remote(source, target, send, recv, group, place):
            return pltpu.make_async_remote_copy(
                src_ref=source,
                dst_ref=target,
                send_sem=send,
                recv_sem=recv,
                device_id=device(group, place),
                device_id_type=pl.DeviceIdType.MESH,
            )

        waits, chains, sums = [], [], []

        def chain_gather(src, dst, sems, sems_two, local, axis, arr):
            name, other = axis
            n, here, m, place = size[name], me[name], size[other], me[other]
            part = arr.shape[0] // m
            rows = pl.ds(pl.multiple_of(place * part, part), part)
            own = pltpu.make_async_copy(src, dst.at[here], local)
            own.start()
            waits.append(own.wait)

            def hop(way, step, source, index):
                to = here + 1 if way == 0 else here - 1
                return remote(
                    source,
                    dst.at[index, rows],
                    sems.at[way, 0, step],
                    sems.at[way, 1, step],
                    name,
                    to,
                )

            def guarded(ok, call):
                waits.append(lambda: pl.when(ok)(call))

            open_ends = (here < n - 1, here > 0)
            for way in range(2):
                @pl.when(open_ends[way])
                def _():
                    hop(way, 0, src.at[rows], here).start()

                guarded(
                    open_ends[way],
                    lambda way=way: hop(way, 0, src.at[rows], here).wait_send(),
                )

            def advance(step):
                for way in range(2):
                    came = here - 1 - step if way == 0 else here + 1 + step
                    ok = came >= 0 if way == 0 else came < n
                    on = jnp.logical_and(ok, open_ends[way])

                    def partners(way=way, came=came):
                        for j in range(1, m):
                            to = lax.rem(place + j, m)
                            whose = lax.rem(place + m - j, m)
                            piece = dst.at[came, rows]
                            theirs = dst.at[came, pl.ds(pl.multiple_of(whose * part, part), part)]
                            send, recv = sems_two.at[way, 0, step, j], sems_two.at[way, 1, step, j]
                            yield (
                                remote(piece, piece, send, recv, other, to),
                                remote(theirs, theirs, send, recv, other, to),
                            )

                    @pl.when(ok)
                    def _():
                        hop(way, step, dst.at[came, rows], came).wait_recv()

                    if step + 1 < n - 1:
                        @pl.when(on)
                        def _():
                            hop(way, step + 1, dst.at[came, rows], came).start()

                        guarded(
                            on,
                            lambda way=way, came=came: hop(
                                way, step + 1, dst.at[came, rows], came
                            ).wait_send(),
                        )

                    @pl.when(ok)
                    def _():
                        for copy, _ in partners():
                            copy.start()

                    def finish(partners=partners):
                        for copy, arrival in partners():
                            copy.wait_send()
                            arrival.wait_recv()

                    guarded(ok, finish)

            chains.append((n - 1, advance, lambda: None))

        def chain_sum(src, dst, sems, sems_two, land, held, axis, arr):
            name, other = axis
            n, here, m, place = size[name], me[name], size[other], me[other]
            tall = 16 if arr.shape[1] % 16 == 0 else arr.shape[1]
            turns = arr.shape[1] // tall

            def by_rows(call):
                def one(turn, carry):
                    call(pl.ds(pl.multiple_of(turn * tall, tall), tall))
                    return carry

                lax.fori_loop(0, turns, one, 0)

            def hop(way, step, source, index):
                to = here + 1 if way == 0 else here - 1
                return remote(
                    source,
                    land.at[way, index],
                    sems.at[way, 0, step],
                    sems.at[way, 1, step],
                    name,
                    to,
                )

            def guarded(ok, call):
                waits.append(lambda: pl.when(ok)(call))

            firsts = (here == 0, here == n - 1)

            def advance(step):
                for way in range(2):
                    goal = n - 1 - step if way == 0 else step
                    passing = here < goal if way == 0 else here > goal
                    inner = jnp.logical_and(passing, jnp.logical_not(firsts[way]))
                    first = jnp.logical_and(passing, firsts[way])

                    @pl.when(first)
                    def _():
                        if step > 0:
                            before = goal + 1 if way == 0 else goal - 1
                            hop(way, step - 1, src.at[before], before).wait_send()
                        hop(way, step, src.at[goal], goal).start()

                    if step == n - 2:
                        guarded(
                            first,
                            lambda way=way, goal=goal: hop(
                                way, step, src.at[goal], goal
                            ).wait_send(),
                        )

                    @pl.when(inner)
                    def _():
                        hop(way, step, land.at[way, goal], goal).wait_recv()

                        def add(rows):
                            held[way, goal, rows] = (
                                land[way, goal, rows].astype(jnp.float32)
                                + src[goal, rows].astype(jnp.float32)
                            ).astype(held.dtype)

                        by_rows(add)
                        hop(way, step, held.at[way, goal], goal).start()

                    guarded(
                        inner,
                        lambda way=way, goal=goal: hop(
                            way, step, held.at[way, goal], goal
                        ).wait_send(),
                    )

            def partners():
                for j in range(1, m):
                    to = lax.rem(place + j, m)
                    whose = lax.rem(place + m - j, m)
                    send, recv = sems_two.at[0, 0, 0, j], sems_two.at[0, 1, 0, j]
                    yield (
                        remote(dst.at[place], dst.at[place], send, recv, other, to),
                        remote(dst.at[whose], dst.at[whose], send, recv, other, to),
                    )

            def close():
                def start(rows):
                    dst[place, rows] = src[here, rows].astype(jnp.float32)

                by_rows(start)
                for way in range(2):
                    step = n - 1 - here if way == 0 else here

                    @pl.when(jnp.logical_not(firsts[way]))
                    def _():
                        hop(way, step, land.at[way, here], here).wait_recv()

                        def add(rows):
                            dst[place, rows] = dst[place, rows] + land[way, here, rows].astype(
                                jnp.float32
                            )

                        by_rows(add)

                for copy, _ in partners():
                    copy.start()
                for copy, arrival in partners():
                    waits.append(copy.wait_send)
                    waits.append(arrival.wait_recv)

            chains.append((n, advance, close))

        for (kind, axis, arr), src, dst in zip(items, ins, outs):
            if kind in ("wg", "rs"):
                extra = [rest.pop(0) for _ in range(3 if kind == "wg" else 4)]
                (chain_gather if kind == "wg" else chain_sum)(src, dst, *extra, axis, arr)
                continue
            sems = rest.pop(0)
            n, here = size[axis], me[axis]
            if kind == "ar":
                sems_two, land = rest.pop(0), rest.pop(0)
                sent = []
                for k in range(1, n):
                    peer = lax.rem(here + k, n)
                    came = lax.rem(here + n - k, n)
                    pair = sems.at[0, k], sems.at[1, k]
                    copy = remote(src.at[peer], land.at[here], *pair, axis, peer)
                    copy.start()
                    sent.append((copy, remote(land.at[came], land.at[came], *pair, axis, peer)))
                sums.append((src, dst, land, sems_two, axis, n, here, sent))
                continue
            local = rest.pop(0)

            def piece(place):
                if kind == "ag":
                    return src
                if isinstance(axis, tuple):
                    return src.at[place // size[axis[1]]]
                return src.at[place]

            own = pltpu.make_async_copy(piece(here), dst.at[here], local)
            own.start()
            waits.append(own.wait)
            for k in range(1, n):
                peer = lax.rem(here + k, n)
                came = lax.rem(here + n - k, n)
                pair = sems.at[0, k], sems.at[1, k]
                copy = remote(piece(peer), dst.at[here], *pair, axis, peer)
                copy.start()
                waits.append(copy.wait_send)
                waits.append(remote(dst.at[came], dst.at[came], *pair, axis, peer).wait_recv)

        def finish_sums():
            for src, dst, land, sems_two, axis, n, here, sent in sums:
                total = src[here].astype(jnp.float32)
                for k, (copy, arrival) in enumerate(sent, 1):
                    arrival.wait_recv()
                    total = total + land[lax.rem(here + n - k, n)].astype(jnp.float32)
                dst[here] = total.astype(dst.dtype)
                for k in range(1, n):
                    peer = lax.rem(here + k, n)
                    came = lax.rem(here + n - k, n)
                    pair = sems_two.at[0, k], sems_two.at[1, k]
                    copy = remote(dst.at[here], dst.at[here], *pair, axis, peer)
                    copy.start()
                    waits.append(copy.wait_send)
                    waits.append(
                        remote(dst.at[came], dst.at[came], *pair, axis, peer).wait_recv
                    )
                for copy, _ in sent:
                    waits.append(copy.wait_send)

        steps = max([entry[0] for entry in chains], default=0)
        for step in range(steps):
            if step == 1:
                finish_sums()
            for last, advance, _ in chains:
                if step < last:
                    advance(step)
        if steps < 2:
            finish_sums()
        for _, _, close in chains:
            close()
        for wait in waits:
            wait()

    def room(shape, dtype):
        item = jnp.dtype(dtype).itemsize
        lead = 1
        for extent in shape[:-2]:
            lead *= extent
        tile = 32 // item
        return lead * (-(-shape[-2] // tile) * tile) * (-(-shape[-1] // 128) * 128) * item

    total = sum(room(item[2].shape, item[2].dtype) for item in items)
    total += sum(room(shape.shape, shape.dtype) for shape in out_shape)
    for kind, _, arr in items:
        total += room(arr.shape, arr.dtype) * {"ar": 3, "rs": 4}.get(kind, 0)
    limit = min(60 * 2**20, total + total // 8 + 2 * 2**20)
    vmem = pl.BlockSpec(memory_space=pltpu.VMEM)
    return pl.pallas_call(
        kernel,
        out_shape=out_shape,
        in_specs=[vmem] * len(items),
        out_specs=[vmem] * len(items),
        scratch_shapes=scratch,
        compiler_params=pltpu.CompilerParams(
            collective_id=cid, has_side_effects=True, vmem_limit_bytes=limit
        ),
    )(*[item[2] for item in items])


def dot_t(left, right):
    return lax.dot_general(
        left, right, (((1,), (1,)), ((), ())), preferred_element_type=jnp.float32
    )


def dot_rows(left, right):
    return lax.dot_general(
        left, right, (((0,), (0,)), ((), ())), preferred_element_type=jnp.float32
    )


def product(left, right):
    return jnp.dot(left, right, preferred_element_type=jnp.float32)


def rms_rows(inputs):
    return lax.rsqrt(jnp.mean(inputs * inputs, axis=-1, keepdims=True) + epsilon)


def norm_back(inputs, scale, gain, grad):
    scaled = gain * grad
    gain_terms = grad * inputs * scale
    input_grad = scale * scaled - inputs * scale**3 * jnp.mean(
        scaled * inputs, axis=-1, keepdims=True
    )
    return (gain_terms, input_grad)


def mixer_block(queries, keys_in, values_in, log_decay, start_state):
    block_len = min(SPAN, queries.shape[0])
    blocks = queries.shape[0] // block_len

    def cut(array):
        return array.reshape(blocks, block_len, array.shape[-1])

    lower = jnp.tril(jnp.ones((block_len, block_len), jnp.float32))

    def block_step(carried, pieces):
        query_blk, key_blk, value_blk, decay_blk = pieces
        running = jnp.cumsum(decay_blk, axis=0)
        from_state = jnp.dot(query_blk * jnp.exp(running), carried, precision=highest)
        spread = (
            jnp.exp(jnp.minimum(running[:, None, :] - running[None, :, :], 0.0)) * lower[:, :, None]
        )
        scores = jnp.einsum("id,jd,ijd->ij", query_blk, key_blk, spread, precision=highest)
        inside = jnp.dot(scores, value_blk, precision=highest)
        ending = running[-1]
        weighted = key_blk * jnp.exp(ending[None, :] - running)
        carried = jnp.exp(ending)[:, None] * carried + jnp.dot(
            weighted.T, value_blk, precision=highest
        )
        return (carried, from_state + inside)

    final_state, outputs = lax.scan(
        jax.checkpoint(block_step),
        start_state,
        (cut(queries), cut(keys_in), cut(values_in), cut(log_decay)),
    )
    return (outputs.reshape(queries.shape[0], values_in.shape[-1]), final_state)


def on_device(
    x_in,
    cotangent,
    attn_gain,
    w_query,
    w_key,
    w_value,
    w_outgate,
    w_lowrank,
    w_forget,
    forget_bias,
    group_gain,
    w_output,
    mlp_gain,
    w_gate,
    w_up,
    w_down,
):
    seqs_here, tok_here, width = x_in.shape
    total_rows = seqs_here * tok_here
    bf16, f32 = jnp.bfloat16, jnp.float32
    n_seq, n_head, n_dp = lax.axis_size("seq"), lax.axis_size("head"), lax.axis_size("dp")
    seq_pos, head_pos = lax.axis_index("seq"), lax.axis_index("head")
    shard_rows = w_query.shape[0]
    part_rows = shard_rows // n_dp
    key_cols, val_cols, hidden = w_query.shape[1], w_value.shape[1], w_gate.shape[1]
    rank = w_lowrank.shape[1]
    heads_here = key_cols // DK
    head_scale = DK ** (-0.5)
    side = -(-(rank + 2) // 128) * 128
    packed = jnp.concatenate(
        (
            w_query,
            w_key,
            w_value,
            w_outgate,
            w_lowrank,
            attn_gain[:, None],
            mlp_gain[:, None],
            jnp.zeros((shard_rows, side - rank - 2), bf16),
            w_output.T,
        ),
        axis=1,
    )
    packed_mlp = jnp.concatenate((w_gate, w_up, w_down.T), axis=1)
    (weights,) = exchange([("wg", ("seq", "dp"), packed)], 0)
    weights = weights.reshape(width, -1)
    attn_cols = 2 * key_cols + 2 * val_cols
    w_attn = weights[:, :attn_cols]
    w_low = weights[:, attn_cols : attn_cols + side]
    wl_full = w_low[:, :rank]
    gain_first = w_low[:, rank].astype(f32)
    gain_second = w_low[:, rank + 1].astype(f32)
    at = attn_cols + side
    wo_t = weights[:, at : at + val_cols]
    forget_cols = lax.dynamic_slice_in_dim(w_forget, head_pos * key_cols, key_cols, 1)
    bias_cols = lax.dynamic_slice_in_dim(forget_bias, head_pos * key_cols, key_cols, 0)

    def heads_of(array, size):
        return array.reshape(seqs_here, tok_here, heads_here, size).transpose(0, 2, 1, 3)

    def rows_of(array):
        return array.transpose(0, 2, 1, 3).reshape(total_rows, -1)

    def spread_head(array):
        return array.astype(bf16).reshape(n_head, array.shape[0] // n_head, array.shape[1])

    def by_part(array):
        array = array.reshape(total_rows, n_seq, n_dp, part_rows)
        return array.transpose(2, 0, 1, 3).reshape(n_dp, total_rows, n_seq * part_rows)

    def all_rows(array):
        return array.reshape(n_dp * total_rows, -1)

    def grad_of(left, right):
        return dot_rows(all_rows(left), all_rows(right)).astype(bf16)

    flat_in = x_in.reshape(total_rows, width)
    flat_cot = cotangent.reshape(total_rows, width)
    scale_one = rms_rows(flat_in)
    normed_in = (flat_in * scale_one * gain_first).astype(bf16)
    proj = product(normed_in, w_attn)
    q_rows = proj[:, :key_cols]
    k_rows = proj[:, key_cols : 2 * key_cols]
    v_rows = proj[:, 2 * key_cols : 2 * key_cols + val_cols]
    og_rows = proj[:, 2 * key_cols + val_cols :]
    low_rank = product(normed_in, wl_full)
    pre_gate = jnp.dot(low_rank, forget_cols, precision=highest) + bias_cols
    log_decay = jax.nn.log_sigmoid(pre_gate) / normalizer
    q_heads = heads_of(q_rows, DK)
    k_heads = heads_of(k_rows, DK)
    v_heads = heads_of(v_rows, DV)
    decay_heads = heads_of(log_decay, DK)
    running = jnp.cumsum(decay_heads, axis=2)
    ending = running[:, :, -1, :]
    decay_total = jnp.exp(ending)
    local_state = jnp.einsum(
        "shld,shlv->shdv",
        k_heads * jnp.exp(ending[:, :, None, :] - running),
        v_heads,
        precision=highest,
    )
    state_shape = local_state.shape
    states, decays = exchange(
        [
            ("ag", "seq", local_state.astype(bf16).reshape(-1, DV)),
            ("ag", "seq", jnp.broadcast_to(decay_total.reshape(1, -1), (8, decay_total.size))),
        ],
        1,
    )
    decays = decays[:, 0].reshape((n_seq,) + decay_total.shape)
    states = states.reshape((n_seq,) + state_shape)
    start_state = jnp.zeros(state_shape, f32)
    for j in range(n_seq - 1):
        start_state = jnp.where(
            j < seq_pos, decays[j][..., None] * start_state + states[j].astype(f32), start_state
        )

    def mixed(q_part, k_part, v_part, d_part):
        return jax.vmap(jax.vmap(mixer_block))(
            q_part * head_scale, k_part, v_part, d_part, start_state
        )

    (o_heads, end_state), pullback = jax.vjp(mixed, q_heads, k_heads, v_heads, decay_heads)
    gate_heads = heads_of(og_rows, DV)
    scale_three = rms_rows(o_heads)
    gated_norm = o_heads * scale_three * group_gain
    gate_sig = jax.nn.sigmoid(gate_heads)
    gate_act = gate_heads * gate_sig
    mixed_out = rows_of(gated_norm * gate_act).astype(bf16)
    mix_sum, weights_mlp = exchange(
        [
            ("ar", "head", spread_head(dot_t(mixed_out, wo_t))),
            ("wg", ("seq", "dp"), packed_mlp),
        ],
        2,
    )
    weights_mlp = weights_mlp.reshape(width, -1)
    w_gu = weights_mlp[:, : 2 * hidden]
    wdown_t = weights_mlp[:, 2 * hidden :]
    resid = flat_in + mix_sum.reshape(total_rows, width).astype(f32)
    scale_two = rms_rows(resid)
    normed_mid = (resid * scale_two * gain_second).astype(bf16)
    both = product(normed_mid, w_gu)
    gate_pre, up_pre = both[:, :hidden], both[:, hidden:]
    gate_sigma = jax.nn.sigmoid(gate_pre)
    gate_silu = gate_pre * gate_sigma
    mlp_hidden = (gate_silu * up_pre).astype(bf16)
    grad_out_b = flat_cot.astype(bf16)
    d_hidden = product(grad_out_b, wdown_t)
    d_gate_pre = (d_hidden * up_pre * gate_sigma * (1.0 + gate_pre * (1.0 - gate_sigma))).astype(
        bf16
    )
    d_up_pre = (d_hidden * gate_silu).astype(bf16)
    d_both = jnp.concatenate((d_gate_pre, d_up_pre), axis=1)
    sums, mid_two, out_two, both_two, hidden_two = exchange(
        [
            (
                "ar",
                "head",
                spread_head(
                    jnp.concatenate((dot_t(mlp_hidden, wdown_t), dot_t(d_both, w_gu)), axis=0)
                ),
            ),
            ("a2a", "dp", by_part(normed_mid)),
            ("a2a", "dp", by_part(grad_out_b)),
            ("ag", "dp", d_both),
            ("ag", "dp", mlp_hidden),
        ],
        3,
    )
    sums = sums.reshape(2, total_rows, width).astype(f32)
    result = resid + sums[0]
    d_normed_mid = sums[1]
    gain_terms, d_resid_norm = norm_back(resid, scale_two, gain_second, d_normed_mid)
    d_gain_two = jnp.sum(gain_terms, axis=0)
    d_resid = flat_cot + d_resid_norm
    d_resid_b = d_resid.astype(bf16)
    d_mixed = heads_of(product(d_resid_b, wo_t), DV)
    d_norm_out = d_mixed * gate_act
    d_gate_heads = d_mixed * gated_norm * gate_sig * (1.0 + gate_heads * (1.0 - gate_sig))
    d_group = jnp.sum(d_norm_out * o_heads * scale_three, axis=(0, 1, 2))
    group_terms, d_o_heads = norm_back(o_heads, scale_three, group_gain, d_norm_out)
    state_grad = jnp.einsum(
        "shld,shlv->shdv", q_heads * head_scale * jnp.exp(running), d_o_heads, precision=highest
    )
    grads_in, mixed_two, resid_two = exchange(
        [
            ("ag", "seq", state_grad.astype(bf16).reshape(-1, DV)),
            ("ag", "dp", mixed_out),
            ("a2a", "dp", by_part(d_resid_b)),
        ],
        4,
    )
    grads_late = jnp.concatenate(
        (
            grad_of(resid_two, mixed_two),
            grad_of(mid_two, both_two),
            grad_of(out_two, hidden_two),
        ),
        axis=1,
    ).reshape(n_seq, part_rows, -1)
    grads_in = grads_in.reshape((n_seq,) + state_shape)
    later_grad = jnp.zeros(state_shape, f32)
    for j in range(n_seq - 1, 0, -1):
        later_grad = jnp.where(
            j > seq_pos, decays[j][..., None] * later_grad + grads_in[j].astype(f32), later_grad
        )
    d_q, d_k, d_v, d_decay = pullback((d_o_heads, later_grad))
    d_pre = rows_of(d_decay) / normalizer * jax.nn.sigmoid(-pre_gate)
    d_bias = jnp.sum(d_pre, axis=0)
    d_forget = jnp.dot(low_rank.T, d_pre, precision=highest)
    d_low_part = jnp.dot(d_pre, forget_cols.T, precision=highest)
    d_proj = jnp.concatenate(
        (
            rows_of(d_q).astype(bf16),
            rows_of(d_k).astype(bf16),
            rows_of(d_v).astype(bf16),
            rows_of(d_gate_heads).astype(bf16),
        ),
        axis=1,
    )
    d_in_part = jnp.concatenate(
        (dot_t(d_proj, w_attn), d_low_part, jnp.zeros((total_rows, side - rank), f32)), axis=1
    )
    group_rows = d_group.reshape(1, DV)
    if DV < key_cols:
        group_rows = jnp.pad(group_rows, ((0, 0), (0, key_cols - DV)))
    if DV > key_cols:
        group_rows = group_rows.reshape(-1, key_cols)
    used = rank + 1 + group_rows.shape[0]
    small = jnp.concatenate(
        (
            d_forget,
            d_bias[None, :],
            group_rows,
            jnp.zeros((-used % 8, key_cols), f32),
        ),
        axis=0,
    )
    grads_late, in_sum, small_all, in_two, proj_two = exchange(
        [
            ("rs", ("seq", "dp"), grads_late),
            ("ar", "head", spread_head(d_in_part)),
            ("ag", ("seq", "dp"), small),
            ("a2a", "dp", by_part(normed_in)),
            ("ag", "dp", d_proj),
        ],
        5,
    )
    in_sum = in_sum.reshape(total_rows, width + side)
    d_low_b = in_sum[:, width : width + rank]
    d_normed_in = in_sum[:, :width].astype(f32) + dot_t(d_low_b, wl_full)
    first_terms, d_in_norm = norm_back(flat_in, scale_one, gain_first, d_normed_in)
    d_gain_one = jnp.sum(first_terms, axis=0)
    grad_in = d_resid + d_in_norm

    grads_attn = grad_of(in_two, proj_two).reshape(n_seq, part_rows, -1)
    tall = jnp.concatenate(
        (
            dot_rows(d_low_b, normed_in),
            d_gain_one[None, :],
            d_gain_two[None, :],
            jnp.zeros((-(rank + 2) % 8, width), f32),
        ),
        axis=0,
    )
    tall = tall.reshape(-1, n_seq, shard_rows).transpose(1, 0, 2)
    grads_attn, tall, small = exchange(
        [
            ("rs", ("seq", "dp"), grads_attn),
            ("a2a", ("seq", "dp"), tall),
            ("ag", "head", jnp.sum(small_all, axis=0)),
        ],
        6,
    )
    grads_attn = grads_attn.reshape(shard_rows, -1)
    grads_late = grads_late.reshape(shard_rows, -1)
    tall = jnp.sum(tall, axis=0)
    s_forget = small[:, :rank].transpose(1, 0, 2).reshape(rank, -1)
    s_bias = small[:, rank].reshape(-1)
    s_group = jnp.sum(small[:, rank + 1 : used], axis=0).reshape(-1)[:DV]
    s_query, s_key, s_value, s_outgate = jnp.split(
        grads_attn, [key_cols, 2 * key_cols, 2 * key_cols + val_cols], axis=1
    )
    s_output, s_gate, s_up, s_down = jnp.split(
        grads_late, [val_cols, val_cols + hidden, val_cols + 2 * hidden], axis=1
    )
    return (
        result.reshape(seqs_here, tok_here, width),
        grad_in.reshape(seqs_here, tok_here, width),
        tall[rank],
        s_query,
        s_key,
        s_value,
        s_outgate,
        tall[:rank].T,
        s_forget,
        s_bias,
        s_group,
        s_output.T,
        tall[rank + 1],
        s_gate,
        s_up,
        s_down.T,
    )


def solution(mesh):
    return jax.shard_map(
        on_device,
        mesh=mesh,
        in_specs=(
            P("dp", "seq", None),
            P("dp", "seq", None),
            P("seq"),
            P("seq", "head"),
            P("seq", "head"),
            P("seq", "head"),
            P("seq", "head"),
            P("seq", None),
            P(),
            P(),
            P(),
            P("head", "seq"),
            P("seq"),
            P("seq", "head"),
            P("seq", "head"),
            P("head", "seq"),
        ),
        out_specs=(
            P("dp", "seq", None),
            P("dp", "seq", None),
            P("seq"),
            P("seq", "head"),
            P("seq", "head"),
            P("seq", "head"),
            P("seq", "head"),
            P("seq", None),
            P(),
            P(),
            P(),
            P("head", "seq"),
            P("seq"),
            P("seq", "head"),
            P("seq", "head"),
            P("head", "seq"),
        ),
        check_vma=False,
    )
```
